32 devices in a mesh: grp: 4 (over x, core), tbl: 8 (over z, y).
Axes of the slice: x: 2, y: 2, z: 4, core: 2. Of those that a mesh axis runs over, the one named last changes fastest.
Arguments:
- cross_input: bfloat16 [4096, 3456], P(('grp', 'tbl')), may hold values from -6 to 6
- upstream: bfloat16 [4096, 3456], P(('grp', 'tbl')), may hold values from -6 to 6
- v_weight: bfloat16 [256, 3456], replicated, may hold values from -0.109375 to 0.109375
- u_weight: bfloat16 [256, 3456], replicated, may hold values from -0.375 to 0.375
- bias: float32 [3456], replicated, may hold values from -3 to 3
- placement: int32 [26], replicated, may hold values from 0 to 7, as said below
- owned_ids: int32 [40, 4, 4096], P('tbl', None, 'grp'), may hold values from 0 to 255
Outputs:
- cross_grad: float32 [256, 6912], P(('grp', 'tbl'))
- table_grad: float32 [40, 256, 128], P('tbl', 'grp')
The draws below stay inside these ranges and needn't reach their ends.
Inputs may be any that keep to these rules, and one draw needn't show every extreme that they name: `placement`: no device holds more than 5 tables, and some device holds exactly 5.
All inputs are finite; a program needn't handle non-finite values.
Results may differ from the reference program's by a relative error of at most 0.004.
Values may be sent and summed in bfloat16 or wider, within the bound.
A program may use at most 64 MiB of HBM per device.

```python
import math
import jax
import jax.numpy as jnp
import numpy as np
from jax import lax

EMB = 128
TABLES = 26
D = 3456
RANK = 256
TOK_DEV = 128
HOT = 4
ROWS = 256
MAXT = 5
SLOTS = 40
TOKENS = 4096
N_TBL = 8
DEVICES = 32


def draw_placement(key, part):
    key_heavy = jax.random.fold_in(key, 11)
    key_score = jax.random.fold_in(key, 12)
    key_order = jax.random.fold_in(key, 13)
    total = N_TBL * MAXT
    heavy = jax.random.randint(key_heavy, (), 0, N_TBL)
    score = jax.random.permutation(key_score, total).astype(jnp.int32)
    slot_ids = jnp.arange(total, dtype=jnp.int32)
    score = jnp.where(slot_ids // MAXT == heavy, total + slot_ids, score)
    unused, chosen = lax.top_k(score, TABLES)
    order = jax.random.permutation(key_order, TABLES)
    return (chosen // MAXT)[order].astype(jnp.int32)


def place_ends(result, own_key, low, high):
    dims = result.shape
    place = [jax.random.randint(jax.random.fold_in(own_key, axis), (), 0, dims[axis]) for axis in range(len(dims))]
    result = result.at[tuple(place)].set(low)
    longest = dims.index(max(dims))
    place[longest] = (place[longest] + 1) % dims[longest]
    return result.at[tuple(place)].set(high)


def level_of(rng, dims, pieces, smallest, top_value):
    level, own = 1.0, jax.random.fold_in(rng, 6)
    for dim, blocks in pieces:
        steps = jnp.exp(jax.random.uniform(jax.random.fold_in(own, dim), (blocks,), jnp.float32, smallest / len(pieces), top_value / len(pieces)))
        level = level * jnp.repeat(steps, dims[dim] // blocks).reshape([-1 if axis == dim else 1 for axis in range(len(dims))])
    return level


def rank_bounds(count, slope):
    portions = [(1 << 20) // math.isqrt(standing ** slope) + 1 for standing in range(1, count + 1)]
    spread = 1 + sum(portions) // (1 << 30)
    return np.cumsum(np.array([max(1, weight // spread) for weight in portions]))


def skewed_ids(rng, shape, number_of, slope):
    grid = rank_bounds(number_of, slope)
    pick = jax.random.randint(jax.random.fold_in(rng, 1), shape, 0, int(grid[number_of - 1]))
    standing = jnp.searchsorted(jnp.asarray(grid, jnp.int32), pick, side="right")
    return jax.random.permutation(jax.random.fold_in(rng, 2), number_of)[standing].astype(jnp.int32)


def centred(rng, shape, scale, bound, pieces=(), held_as=jnp.bfloat16):
    drawn = jax.random.normal(rng, shape, jnp.float32) * scale
    if len(pieces) > 0:
        drawn = level_of(rng, shape, pieces, -0.22, 0.18) * drawn
    return jnp.clip(drawn, min=-bound, max=bound).astype(held_as)


def setup_inputs(seed: int = 0) -> dict:
    streams_of = jax.random.split(jax.random.key(seed), 8)
    return {
        "cross_input": centred(streams_of[0], (TOKENS, D), 1.0, 6.0, ((0, 32),)),
        "upstream": centred(streams_of[1], (TOKENS, D), 1.0, 6.0, ((0, 32),)),
        "v_weight": centred(streams_of[2], (RANK, D), D ** -0.5, 0.109375),
        "u_weight": centred(streams_of[3], (RANK, D), RANK ** -0.5, 0.375),
        "bias": centred(streams_of[4], (D,), 0.5, 3.0, (), jnp.float32),
        "placement": draw_placement(jax.random.fold_in(streams_of[7], 71), 0),
        "owned_ids": place_ends(skewed_ids(streams_of[6], (SLOTS, HOT, TOKENS), ROWS, 1), jax.random.fold_in(streams_of[6], 3), 0, ROWS - 1).astype(jnp.int32),
    }


def block_terms(cross_input, upstream, v_weight, u_weight, bias):
    hidden = jnp.dot(cross_input, v_weight.T, preferred_element_type=jnp.float32).astype(jnp.bfloat16)
    mixed = jnp.dot(hidden, u_weight, preferred_element_type=jnp.float32) + bias
    up_float = upstream.astype(jnp.float32)
    product_grad = (up_float * cross_input.astype(jnp.float32)).astype(jnp.bfloat16)
    grad_u = jnp.dot(hidden.T, product_grad, preferred_element_type=jnp.float32)
    hidden_grad = jnp.dot(product_grad, u_weight.T, preferred_element_type=jnp.float32).astype(jnp.bfloat16)
    grad_v = jnp.dot(hidden_grad.T, cross_input, preferred_element_type=jnp.float32)
    input_grad = up_float * (1.0 + mixed) + jnp.dot(hidden_grad, v_weight, preferred_element_type=jnp.float32)
    pooled = input_grad[:, EMB:].astype(jnp.bfloat16)
    return (grad_u, grad_v, pooled)

def reference(cross_input, upstream, v_weight, u_weight, bias, placement, owned_ids):
    inputs_blocks = cross_input.reshape(DEVICES, TOK_DEV, D)
    upstream_blocks = upstream.reshape(DEVICES, TOK_DEV, D)

    def advance(carry, item):
        grad_u, grad_v, pooled = block_terms(item[0], item[1], v_weight, u_weight, bias)
        return ((carry[0] + grad_u, carry[1] + grad_v), pooled)
    start = (jnp.zeros((RANK, D), jnp.float32), jnp.zeros((RANK, D), jnp.float32))
    sums, pooled = lax.scan(advance, start, (inputs_blocks, upstream_blocks))
    cross_grad = jnp.concatenate([sums[0], sums[1]], axis=1) * (1.0 / math.sqrt(TOKENS))
    pooled = pooled.reshape(TOKENS, TABLES, EMB)
    same = placement[:, None] == placement[None, :]
    earlier = jnp.arange(TABLES)[None, :] < jnp.arange(TABLES)[:, None]
    slot = lax.optimization_barrier(jnp.sum((same & earlier).astype(jnp.int32), axis=1)).astype(jnp.int32)
    target = (placement * MAXT + slot).astype(jnp.int32)
    table_grad = jnp.zeros((SLOTS, ROWS, EMB), jnp.float32)
    for table in range(TABLES):
        values = pooled[:, table, :].astype(jnp.float32)
        row_ids = owned_ids[target[table]]
        total = jnp.zeros((ROWS, EMB), jnp.float32)
        for lookup in range(HOT):
            total = total + jax.ops.segment_sum(values, row_ids[lookup], num_segments=ROWS)
        table_grad = table_grad.at[target[table]].add(total)
    return (cross_grad, table_grad)
```

```python
import functools
import math

import jax
import jax.numpy as jnp
from jax import lax
from jax.experimental import pallas as pl
from jax.experimental.pallas import tpu as pltpu
from jax.sharding import PartitionSpec as P

EMB = 128
TABLES = 26
ROWS = 256
MESH = pl.DeviceIdType.MESH


def outer_sum(left, right):
    return jnp.einsum("br,bd->rd", left, right, preferred_element_type=jnp.float32)


def on_device(cross_input, upstream, v_weight, u_weight, bias, placement, owned_ids):
    n_grp = lax.axis_size("grp")
    n_tbl = lax.axis_size("tbl")
    samples = cross_input.shape[0]
    slots_dev = owned_ids.shape[0]
    scale = 1.0 / math.sqrt(samples * n_grp * n_tbl)
    hidden = jnp.dot(cross_input, v_weight.T, preferred_element_type=jnp.float32).astype(
        jnp.bfloat16
    )
    mixed = jnp.dot(hidden, u_weight, preferred_element_type=jnp.float32) + bias
    up_float = upstream.astype(jnp.float32)
    product_grad = (up_float * cross_input.astype(jnp.float32)).astype(jnp.bfloat16)
    hidden_grad = jnp.dot(product_grad, u_weight.T, preferred_element_type=jnp.float32).astype(
        jnp.bfloat16
    )
    input_grad = up_float * (1.0 + mixed) + jnp.dot(
        hidden_grad, v_weight, preferred_element_type=jnp.float32
    )
    pooled = input_grad[:, EMB:].astype(jnp.bfloat16).reshape(samples, TABLES, EMB)
    same = placement[:, None] == placement[None, :]
    earlier = jnp.arange(TABLES)[None, :] < jnp.arange(TABLES)[:, None]
    slot = jnp.sum((same & earlier).astype(jnp.int32), axis=1)
    target = slot * n_tbl + placement
    select = (jnp.arange(slots_dev * n_tbl, dtype=jnp.int32)[:, None] == target[None, :]).astype(
        jnp.bfloat16
    )
    outgoing = jnp.einsum("st,bte->sbe", select, pooled, preferred_element_type=jnp.float32)
    outgoing = outgoing.astype(jnp.bfloat16).reshape(slots_dev, n_tbl, samples, EMB)
    arriving = lax.all_to_all(outgoing, "tbl", split_axis=1, concat_axis=1, tiled=True)
    arriving = arriving.reshape(slots_dev, n_tbl * samples, EMB)
    row_numbers = jnp.arange(ROWS, dtype=jnp.int32)
    counts = jnp.sum(
        (owned_ids[:, :, None, :] == row_numbers[None, None, :, None]).astype(jnp.bfloat16), axis=1
    )
    row_terms = jnp.einsum("srm,sme->sre", counts, arriving, preferred_element_type=jnp.float32)
    table_grad = lax.psum_scatter(row_terms, "grp", scatter_dimension=1, tiled=True)
    term = jnp.concatenate(
        [outer_sum(hidden, product_grad), outer_sum(hidden_grad, cross_input)], axis=1
    )
    summed = lax.psum_scatter(term, ("grp", "tbl"), scatter_dimension=0, tiled=True)
    cross_grad = summed * scale
    return (cross_grad, table_grad)


def flip_stages(n_grp, n_tbl):
    return n_grp == 4 and n_tbl == 8


def fused_body(
    n_grp, n_tbl, scale, cut,
    ci_ref, up_ref, v_ref, u_ref, bias_ref, place_ref, inv_ref, ids_ref,
    cross_ref, table_ref,
    ci2, up2, pg, hid, hgr, hid_t, hgr_t, ids_in,
    sa, sb, st, ra1, ra2, ra3, ra4, rb1, rb2, rb3, rb4, rt1, rt2, rt3, rt4,
    pa1, pa2, pa3, pb1, pb2, pb3, pt1, pte, pt2, pt3,
    ssem, rsem, in_ssem, in_rsem, id_ssem, id_rsem,
):
    f32, bf16 = jnp.float32, jnp.bfloat16
    g = lax.axis_index("grp")
    t = lax.axis_index("tbl")
    core, x = g % 2, g // 2
    y, zl, zh = t % 2, (t // 2) % 2, t // 4
    og = g + 1 - 2 * core
    xg = core + 2 * (1 - x)
    yt = t + 1 - 2 * y
    zlt = t + 2 * (1 - 2 * zl)
    zht = t + 4 * (1 - 2 * zh)
    samples, width = ci_ref.shape
    rank = v_ref.shape[0]
    slots_dev = ids_ref.shape[0]
    part = ROWS // n_grp

    barrier = pltpu.get_barrier_semaphore()

    def greet(gg, tt):
        pl.semaphore_signal(barrier, inc=1, device_id=(gg, tt), device_id_type=MESH)

    for step in range(1, n_tbl):
        greet(g, (t + step) % n_tbl)
        greet(og, (t + step) % n_tbl)
    greet(og, t)
    greet(xg, t)
    pl.semaphore_wait(barrier, 2 * n_tbl)

    def send(src, dst, s, r, gg, tt):
        copy = pltpu.make_async_remote_copy(
            src_ref=src, dst_ref=dst, send_sem=s, recv_sem=r,
            device_id=(gg, tt), device_id_type=MESH,
        )
        copy.start()
        return copy

    in_copies = [
        send(ci_ref, ci2, in_ssem.at[0], in_rsem.at[0], og, t),
        send(up_ref, up2, in_ssem.at[1], in_rsem.at[1], og, t),
    ]
    id_copies = []
    for step in range(n_tbl):
        to = (t + step) % n_tbl
        block = ids_ref.at[:, :, pl.ds(pl.multiple_of(to * samples, samples), samples)]
        if step == 0:
            mine = pltpu.make_async_copy(block, ids_in.at[0, t], id_ssem.at[0, 0])
            mine.start()
        else:
            id_copies.append(
                send(block, ids_in.at[0, t], id_ssem.at[0, step], id_rsem.at[0, step], g, to)
            )
        id_copies.append(
            send(block, ids_in.at[1, t], id_ssem.at[1, step], id_rsem.at[1, step], og, to)
        )

    nt = (((1,), (1,)), ((), ()))

    def forward(c_in, u_in, row):
        rows = pl.ds(row, samples)
        hidden = lax.dot_general(c_in[...], v_ref[...], nt, preferred_element_type=f32)
        hid[rows, :] = hidden.astype(bf16)
        hid_t[:, rows] = hidden.T.astype(bf16)
        pg[rows, :] = (u_in[...].astype(f32) * c_in[...].astype(f32)).astype(bf16)
        hgrad = lax.dot_general(pg[rows, :], u_ref[...], nt, preferred_element_type=f32)
        hgr[rows, :] = hgrad.astype(bf16)
        hgr_t[:, rows] = hgrad.T.astype(bf16)

    forward(ci_ref, up_ref, 0)
    for copy in in_copies:
        copy.wait()
    forward(ci2, up2, samples)

    quarter = rank // n_grp

    def picked(ref):
        low = ref[pl.ds(pl.multiple_of(core * quarter, quarter), quarter), :]
        high = ref[pl.ds(pl.multiple_of((core + 2) * quarter, quarter), quarter), :]
        return jnp.concatenate([low, high], axis=0)

    hsel, gsel = picked(hid_t), picked(hgr_t)

    def outer(dst, start, stop):
        for lo in range(start, stop, 512):
            hi = min(lo + 512, stop)
            left = jnp.dot(hsel, pg[:, lo:hi], preferred_element_type=f32)
            right = jnp.dot(gsel[:, :samples], ci_ref[:, lo:hi], preferred_element_type=f32)
            right += jnp.dot(gsel[:, samples:], ci2[:, lo:hi], preferred_element_type=f32)
            for d in range(2 * n_tbl):
                both = jnp.concatenate([left[8 * d : 8 * d + 8], right[8 * d : 8 * d + 8]], axis=0)
                tt = d % n_tbl
                dst[d // n_tbl, tt // 4, (tt // 2) % 2, tt % 2, :, lo - start : hi - start] = (
                    both.astype(bf16)
                )

    outer(sa, 0, cut)
    a1 = send(sa.at[1 - x], ra1, ssem.at[0], rsem.at[0], xg, t)
    outer(sb, cut, width)
    b1 = send(sb.at[:, :, :, 1 - y], rb1, ssem.at[1], rsem.at[1], g, yt)

    mine.wait()
    for copy in id_copies:
        copy.wait()

    index = lax.broadcasted_iota(jnp.int32, (2 * part, samples), 0)
    row_of = (index // part * 2 + core) * part + index % part

    def tables(pair, carry):
        base = pl.multiple_of(EMB + pair * 2 * EMB, EMB)
        cols = pl.ds(base, 2 * EMB)
        mixed = jnp.dot(hid[...], u_ref[:, cols], preferred_element_type=f32) + bias_ref[:, cols]
        back = jnp.dot(hgr[...], v_ref[:, cols], preferred_element_type=f32)
        up_all = jnp.concatenate([up_ref[:, cols], up2[:, cols]], axis=0).astype(f32)
        pooled = (up_all * (1.0 + mixed) + back).astype(bf16)
        for half in range(2):
            table = pair * 2 + half
            owner, slot = place_ref[0, table], place_ref[1, table]
            sums = jnp.zeros((2 * part, EMB), f32)
            for who in range(2):
                looked = ids_in[who, owner, slot]
                count = jnp.zeros((2 * part, samples), f32)
                for k in range(looked.shape[0]):
                    count += jnp.where(looked[k : k + 1, :] == row_of, 1.0, 0.0)
                sums += jnp.dot(
                    count.astype(bf16),
                    pooled[who * samples : (who + 1) * samples, half * EMB : (half + 1) * EMB],
                    preferred_element_type=f32,
                )
            st[0, table] = sums[:part].astype(bf16)
            st[1, table] = sums[part:].astype(bf16)
        return carry

    def plus(p, q):
        return p.astype(f32) + q.astype(f32)

    half_pairs = TABLES // 4
    lax.fori_loop(0, half_pairs, tables, 0)

    a1.wait()
    for i in range(2):
        for j in range(2):
            for k in range(2):
                pa1[i, j, k] = plus(sa[x, i, j, k], ra1[i, j, k]).astype(bf16)
    a2 = send(pa1.at[:, :, 1 - y], ra2, ssem.at[2], rsem.at[2], g, yt)

    lax.fori_loop(half_pairs, TABLES // 2, tables, 0)
    t1 = send(st.at[1 - x], rt1, ssem.at[3], rsem.at[3], xg, t)

    b1.wait()
    for i in range(2):
        for j in range(2):
            for k in range(2):
                pb1[i, j, k] = plus(sb[i, j, k, y], rb1[i, j, k]).astype(bf16)
    b2 = send(pb1.at[1 - x], rb2, ssem.at[4], rsem.at[4], xg, t)

    a2.wait()
    for i in range(2):
        for j in range(2):
            pa2[i, j] = plus(pa1[i, j, y], ra2[i, j]).astype(bf16)
    a3 = send(pa2.at[:, 1 - zl], ra3, ssem.at[5], rsem.at[5], g, zlt)

    t1.wait()

    def add_table(i, carry):
        pt1[i] = plus(st[x, i], rt1[i])
        return carry

    lax.fori_loop(0, TABLES, add_table, 0)

    def expand(i, carry):
        which = inv_ref[i]
        there = jnp.where(which >= 0, 1.0, 0.0)
        owner, slot = i // slots_dev, i % slots_dev
        pte[owner // 4, (owner // 2) % 2, owner % 2, slot] = (
            pt1[jnp.maximum(which, 0)] * there
        ).astype(bf16)
        return carry

    lax.fori_loop(0, slots_dev * n_tbl, expand, 0)
    t2 = send(pte.at[:, :, 1 - y], rt2, ssem.at[6], rsem.at[6], g, yt)

    b2.wait()
    for i in range(2):
        for j in range(2):
            pb2[i, j] = plus(pb1[x, i, j], rb2[i, j]).astype(bf16)
    b3 = send(pb2.at[:, 1 - zl], rb3, ssem.at[7], rsem.at[7], g, zlt)

    a3.wait()
    for i in range(2):
        pa3[i] = plus(pa2[i, zl], ra3[i]).astype(bf16)
    a4 = send(pa3.at[1 - zh], ra4, ssem.at[8], rsem.at[8], g, zht)

    b3.wait()
    for i in range(2):
        pb3[i] = plus(pb2[i, zl], rb3[i]).astype(bf16)
    b4 = send(pb3.at[1 - zh], rb4, ssem.at[9], rsem.at[9], g, zht)

    t2.wait()
    for i in range(2):
        for j in range(2):
            pt2[i, j] = plus(pte[i, j, y], rt2[i, j]).astype(bf16)
    t3 = send(pt2.at[:, 1 - zl], rt3, ssem.at[10], rsem.at[10], g, zlt)

    def finish(value, lo, hi):
        value = value * scale
        cross_ref[:, lo:hi] = value[:8]
        cross_ref[:, width + lo : width + hi] = value[8:]

    a4.wait()
    finish(plus(pa3[zh], ra4[...]), 0, cut)
    b4.wait()
    finish(plus(pb3[zh], rb4[...]), cut, width)
    t3.wait()
    for i in range(2):
        pt3[i] = plus(pt2[i, zl], rt3[i]).astype(bf16)
    t4 = send(pt3.at[1 - zh], rt4, ssem.at[11], rsem.at[11], g, zht)
    t4.wait()
    table_ref[...] = plus(pt3[zh], rt4[...])


def on_device_fused(cross_input, upstream, v_weight, u_weight, bias, placement, owned_ids):
    n_grp = lax.axis_size("grp")
    n_tbl = lax.axis_size("tbl")
    samples, width = cross_input.shape
    rank = v_weight.shape[0]
    slots_dev, hot = owned_ids.shape[:2]
    scale = 1.0 / math.sqrt(samples * n_grp * n_tbl)
    order = jnp.arange(TABLES, dtype=jnp.int32)
    same = placement[:, None] == placement[None, :]
    slot = jnp.sum((same & (order[None, :] < order[:, None])).astype(jnp.int32), axis=1)
    places = jnp.stack([placement, slot])
    hit = jnp.arange(slots_dev * n_tbl, dtype=jnp.int32)[:, None] == (placement * slots_dev + slot)
    inverse = jnp.max(jnp.where(hit, order[None, :], -1), axis=1)
    part = ROWS // n_grp
    cut = (width // EMB * 2 // 5) * EMB
    rest = width - cut
    bf16, f32, i32 = jnp.bfloat16, jnp.float32, jnp.int32
    V = pltpu.VMEM
    tab = (slots_dev, part, EMB)
    scratch = [
        V((samples, width), bf16), V((samples, width), bf16), V((2 * samples, width), bf16),
        V((2 * samples, rank), bf16), V((2 * samples, rank), bf16),
        V((rank, 2 * samples), bf16), V((rank, 2 * samples), bf16),
        V((2, n_tbl, slots_dev, hot, samples), i32),
        V((2, 2, 2, 2, 16, cut), bf16), V((2, 2, 2, 2, 16, rest), bf16),
        V((2, TABLES, part, EMB), bf16),
        V((2, 2, 2, 16, cut), bf16), V((2, 2, 16, cut), bf16), V((2, 16, cut), bf16), V((16, cut), bf16),
        V((2, 2, 2, 16, rest), bf16), V((2, 2, 16, rest), bf16), V((2, 16, rest), bf16), V((16, rest), bf16),
        V((TABLES, part, EMB), bf16), V((2, 2, *tab), bf16), V((2, *tab), bf16), V(tab, bf16),
        V((2, 2, 2, 16, cut), bf16), V((2, 2, 16, cut), bf16), V((2, 16, cut), bf16),
        V((2, 2, 2, 16, rest), bf16), V((2, 2, 16, rest), bf16), V((2, 16, rest), bf16),
        V((TABLES, part, EMB), f32), V((2, 2, 2, *tab), bf16), V((2, 2, *tab), bf16), V((2, *tab), bf16),
        pltpu.SemaphoreType.DMA((12,)), pltpu.SemaphoreType.DMA((12,)),
        pltpu.SemaphoreType.DMA((2,)), pltpu.SemaphoreType.DMA((2,)),
        pltpu.SemaphoreType.DMA((2, n_tbl)), pltpu.SemaphoreType.DMA((2, n_tbl)),
    ]
    vmem = pl.BlockSpec(memory_space=pltpu.VMEM)
    smem = pl.BlockSpec(memory_space=pltpu.SMEM)
    return pl.pallas_call(
        functools.partial(fused_body, n_grp, n_tbl, scale, cut),
        out_shape=(
            jax.ShapeDtypeStruct((2 * rank // (n_grp * n_tbl) // 2, 2 * width), f32),
            jax.ShapeDtypeStruct(tab, f32),
        ),
        in_specs=[vmem] * 5 + [smem] * 2 + [vmem],
        out_specs=(vmem, vmem),
        scratch_shapes=scratch,
        compiler_params=pltpu.CompilerParams(
            collective_id=0, has_side_effects=True, vmem_limit_bytes=60 * 1024 * 1024
        ),
        name="cross_backward",
    )(cross_input, upstream, v_weight, u_weight, bias[None, :], places, inverse, owned_ids)


def solution(mesh):
    in_specs = (
        P(("grp", "tbl"), None),
        P(("grp", "tbl"), None),
        P(),
        P(),
        P(),
        P(),
        P("tbl", None, "grp"),
    )
    out_specs = (P(("grp", "tbl"), None), P("tbl", "grp", None))
    sizes = mesh.shape
    fused = flip_stages(sizes["grp"], sizes["tbl"])
    return jax.shard_map(
        on_device_fused if fused else on_device, mesh=mesh, in_specs=in_specs, out_specs=out_specs, check_vma=False
    )
```

```python
import functools
import math

import jax
import jax.numpy as jnp
from jax import lax
from jax.experimental import pallas as pl
from jax.experimental.pallas import tpu as pltpu
from jax.sharding import PartitionSpec as P

EMB = 128
TABLES = 26
ROWS = 256
MESH = pl.DeviceIdType.MESH


def outer_sum(left, right):
    return jnp.einsum("br,bd->rd", left, right, preferred_element_type=jnp.float32)


def on_device(cross_input, upstream, v_weight, u_weight, bias, placement, owned_ids):
    n_grp = lax.axis_size("grp")
    n_tbl = lax.axis_size("tbl")
    samples = cross_input.shape[0]
    slots_dev = owned_ids.shape[0]
    scale = 1.0 / math.sqrt(samples * n_grp * n_tbl)
    hidden = jnp.dot(cross_input, v_weight.T, preferred_element_type=jnp.float32).astype(
        jnp.bfloat16
    )
    mixed = jnp.dot(hidden, u_weight, preferred_element_type=jnp.float32) + bias
    up_float = upstream.astype(jnp.float32)
    product_grad = (up_float * cross_input.astype(jnp.float32)).astype(jnp.bfloat16)
    hidden_grad = jnp.dot(product_grad, u_weight.T, preferred_element_type=jnp.float32).astype(
        jnp.bfloat16
    )
    input_grad = up_float * (1.0 + mixed) + jnp.dot(
        hidden_grad, v_weight, preferred_element_type=jnp.float32
    )
    pooled = input_grad[:, EMB:].astype(jnp.bfloat16).reshape(samples, TABLES, EMB)
    same = placement[:, None] == placement[None, :]
    earlier = jnp.arange(TABLES)[None, :] < jnp.arange(TABLES)[:, None]
    slot = jnp.sum((same & earlier).astype(jnp.int32), axis=1)
    target = slot * n_tbl + placement
    select = (jnp.arange(slots_dev * n_tbl, dtype=jnp.int32)[:, None] == target[None, :]).astype(
        jnp.bfloat16
    )
    outgoing = jnp.einsum("st,bte->sbe", select, pooled, preferred_element_type=jnp.float32)
    outgoing = outgoing.astype(jnp.bfloat16).reshape(slots_dev, n_tbl, samples, EMB)
    arriving = lax.all_to_all(outgoing, "tbl", split_axis=1, concat_axis=1, tiled=True)
    arriving = arriving.reshape(slots_dev, n_tbl * samples, EMB)
    row_numbers = jnp.arange(ROWS, dtype=jnp.int32)
    counts = jnp.sum(
        (owned_ids[:, :, None, :] == row_numbers[None, None, :, None]).astype(jnp.bfloat16), axis=1
    )
    row_terms = jnp.einsum("srm,sme->sre", counts, arriving, preferred_element_type=jnp.float32)
    table_grad = lax.psum_scatter(row_terms, "grp", scatter_dimension=1, tiled=True)
    term = jnp.concatenate(
        [outer_sum(hidden, product_grad), outer_sum(hidden_grad, cross_input)], axis=1
    )
    summed = lax.psum_scatter(term, ("grp", "tbl"), scatter_dimension=0, tiled=True)
    cross_grad = summed * scale
    return (cross_grad, table_grad)


def halving_fits(n_grp, n_tbl):
    return n_grp == 4 and n_tbl == 8


def scratch_of(samples, width, rank, n_tbl, slots_dev, hot, part, cut):
    f32, bf16, i32 = jnp.float32, jnp.bfloat16, jnp.int32
    V, rest, half = pltpu.VMEM, width - cut, part // 2
    tab = (slots_dev, half, EMB)
    out = {
        "ci": V((2, samples, width), bf16),
        "up": V((2, samples, width), bf16),
        "v": V((rank, width), bf16),
        "u": V((rank, width), bf16),
        "pg": V((2 * samples, width), bf16),
        "hid": V((2 * samples, rank), bf16),
        "hgr": V((2 * samples, rank), bf16),
        "hid_t": V((rank, 2 * samples), bf16),
        "hgr_t": V((rank, 2 * samples), bf16),
        "ids": V((2, n_tbl, slots_dev, hot, samples), i32),
        "pt": V((2, TABLES, half, EMB), f32),
        "slot": pltpu.SMEM((TABLES,), i32),
        "inv": pltpu.SMEM((slots_dev * n_tbl,), i32),
        "load_sem": pltpu.SemaphoreType.DMA((4,)),
        "in_s": pltpu.SemaphoreType.DMA((2,)),
        "in_r": pltpu.SemaphoreType.DMA((2,)),
        "id_s": pltpu.SemaphoreType.DMA((2, n_tbl)),
        "id_r": pltpu.SemaphoreType.DMA((2, n_tbl)),
        "ssem": pltpu.SemaphoreType.DMA((16,)),
        "rsem": pltpu.SemaphoreType.DMA((16,)),
    }
    lead = ((2, 2, 2), (2, 2), (2,), ())
    for name, first, tile in (
        ("a", (2, 2, 2), (16, cut)),
        ("b", (2, 2, 2), (16, rest)),
        ("c", None, tab),
        ("d", (2, 2, 2), tab),
    ):
        for k in range(4):
            shape = lead[k] + tile
            if name == "c" and k == 0:
                shape = (TABLES, half, EMB)
            out["s%s%d" % (name, k)] = V(shape, bf16)
            out["r%s%d" % (name, k)] = V(shape, bf16)
            out["o%s%d" % (name, k)] = V(shape, f32)
    return out


def fused_body(n_grp, n_tbl, scale, cut, names, *refs):
    f32, bf16 = jnp.float32, jnp.bfloat16
    ci_hbm, up_hbm, v_hbm, u_hbm, bias_ref, place_ref, ids_hbm, cross_ref, table_ref = refs[:9]
    r = dict(zip(names, refs[9:]))
    g = lax.axis_index("grp")
    t = lax.axis_index("tbl")
    core, x = g % 2, g // 2
    y, zl, zh = t % 2, (t // 2) % 2, t // 4
    og = g + 1 - 2 * core
    xg = core + 2 * (1 - x)
    yt = t + 1 - 2 * y
    zlt = t + 2 * (1 - 2 * zl)
    zht = t + 4 * (1 - 2 * zh)
    samples, width = ci_hbm.shape
    rank = v_hbm.shape[0]
    slots_dev = ids_hbm.shape[0]
    part = ROWS // n_grp
    half = part // 2

    barrier = pltpu.get_barrier_semaphore()

    def greet(gg, tt):
        pl.semaphore_signal(barrier, inc=1, device_id=(gg, tt), device_id_type=MESH)

    for step in range(1, n_tbl):
        greet(g, (t + step) % n_tbl)
        greet(og, (t + step) % n_tbl)
    greet(og, t)
    greet(xg, t)

    loads = [
        pltpu.make_async_copy(src, dst, r["load_sem"].at[i])
        for i, (src, dst) in enumerate(
            ((ci_hbm, r["ci"].at[0]), (v_hbm, r["v"]), (up_hbm, r["up"].at[0]), (u_hbm, r["u"]))
        )
    ]
    for load in loads:
        load.start()

    places = [place_ref[i] for i in range(TABLES)]
    targets = []
    for i in range(TABLES):
        slot = jnp.int32(0)
        for j in range(i):
            slot += (places[j] == places[i]).astype(jnp.int32)
        r["slot"][i] = jnp.minimum(slot, slots_dev - 1)
        targets.append(places[i] * slots_dev + slot)
    for q in range(slots_dev * n_tbl):
        which = jnp.int32(-1)
        for i in range(TABLES):
            which = jnp.where(targets[i] == q, i, which)
        r["inv"][q] = which

    pl.semaphore_wait(barrier, 2 * n_tbl)

    def remote(src, dst, s, rs, gg, tt):
        copy = pltpu.make_async_remote_copy(
            src_ref=src, dst_ref=dst, send_sem=s, recv_sem=rs,
            device_id=(gg, tt), device_id_type=MESH,
        )
        copy.start()
        return copy

    in_copies = [
        remote(ci_hbm, r["ci"].at[1], r["in_s"].at[0], r["in_r"].at[0], og, t),
        remote(up_hbm, r["up"].at[1], r["in_s"].at[1], r["in_r"].at[1], og, t),
    ]
    id_copies = []
    for step in range(n_tbl):
        to = (t + step) % n_tbl
        block = ids_hbm.at[:, :, pl.ds(pl.multiple_of(to * samples, samples), samples)]
        if step == 0:
            mine = pltpu.make_async_copy(block, r["ids"].at[0, t], r["id_s"].at[0, 0])
            mine.start()
        else:
            id_copies.append(
                remote(block, r["ids"].at[0, t], r["id_s"].at[0, step], r["id_r"].at[0, step], g, to)
            )
        id_copies.append(
            remote(block, r["ids"].at[1, t], r["id_s"].at[1, step], r["id_r"].at[1, step], og, to)
        )

    nt = (((1,), (1,)), ((), ()))

    def forward(who):
        row = who * samples
        rows = pl.ds(row, samples)
        if who == 0:
            loads[0].wait()
            loads[1].wait()
        else:
            in_copies[0].wait()
        hidden = lax.dot_general(r["ci"][who], r["v"][...], nt, preferred_element_type=f32)
        r["hid"][rows, :] = hidden.astype(bf16)
        r["hid_t"][:, rows] = hidden.T.astype(bf16)
        if who == 0:
            loads[2].wait()
            loads[3].wait()
        else:
            in_copies[1].wait()
        r["pg"][rows, :] = (r["up"][who].astype(f32) * r["ci"][who].astype(f32)).astype(bf16)
        hgrad = lax.dot_general(r["pg"][rows, :], r["u"][...], nt, preferred_element_type=f32)
        r["hgr"][rows, :] = hgrad.astype(bf16)
        r["hgr_t"][:, rows] = hgrad.T.astype(bf16)

    forward(0)
    forward(1)

    quarter = rank // n_grp

    def picked(ref):
        mine_rows = ref[pl.ds(pl.multiple_of((core + 2 * x) * quarter, quarter), quarter), :]
        other_rows = ref[pl.ds(pl.multiple_of((core + 2 - 2 * x) * quarter, quarter), quarter), :]
        return jnp.concatenate([mine_rows, other_rows], axis=0)

    hsel, gsel = picked(r["hid_t"]), picked(r["hgr_t"])

    def blocks(lo, hi):
        left = jnp.dot(hsel, r["pg"][:, lo:hi], preferred_element_type=f32)
        right = jnp.dot(gsel[:, :samples], r["ci"][0, :, lo:hi], preferred_element_type=f32)
        right += jnp.dot(gsel[:, samples:], r["ci"][1, :, lo:hi], preferred_element_type=f32)
        return [
            jnp.concatenate([left[8 * d : 8 * d + 8], right[8 * d : 8 * d + 8]], axis=0)
            for d in range(2 * n_tbl)
        ]

    for lo in range(0, cut, 512):
        hi = min(lo + 512, cut)
        made = blocks(lo, hi)
        for d in range(n_tbl):
            at = (d // 4, (d // 2) % 2, d % 2, slice(None), slice(lo, hi))
            r["oa0"][at] = made[d]
            r["sa0"][at] = made[n_tbl + d].astype(bf16)
    sems = iter(range(16))

    def send(name, k, gg, tt):
        i = next(sems)
        return remote(
            r["s%s%d" % (name, k)], r["r%s%d" % (name, k)], r["ssem"].at[i], r["rsem"].at[i], gg, tt
        )

    a0 = send("a", 0, xg, t)
    for lo in range(cut, width, 512):
        hi = min(lo + 512, width)
        made = blocks(lo, hi)
        for side in range(2):
            xx = x if side == 0 else 1 - x
            for z in range(n_tbl // 2):
                even, odd = made[side * n_tbl + 2 * z], made[side * n_tbl + 2 * z + 1]
                at = (xx, z // 2, z % 2, slice(None), slice(lo - cut, hi - cut))
                r["ob0"][at] = jnp.where(y == 0, even, odd)
                r["sb0"][at] = jnp.where(y == 0, odd, even).astype(bf16)
    b0 = send("b", 0, g, yt)

    def indices(depth):
        out = [()]
        for _ in range(depth):
            out = [i + (j,) for i in out for j in range(2)]
        return out

    def halve(name, k, axis, bit, gg, tt, before):
        before.wait()
        own, came = r["o%s%d" % (name, k)], r["r%s%d" % (name, k)]
        kept, out = r["o%s%d" % (name, k + 1)], r["s%s%d" % (name, k + 1)]

        def where_to(i, b):
            return i[:axis] + (b,) + i[axis:]

        def fill(dst, b, kind):
            for i in indices(2 - k):
                at = where_to(i, b)
                value = own[at] + came[at].astype(f32)
                if i:
                    dst[i] = value.astype(kind)
                else:
                    dst[...] = value.astype(kind)

        fill(out, 1 - bit, bf16)
        copy = send(name, k + 1, gg, tt)
        fill(kept, bit, f32)
        return copy

    index = lax.broadcasted_iota(jnp.int32, (2 * part, samples), 0)
    side_of = jnp.where(index // part == 0, x, 1 - x)
    row_of = (side_of * 2 + core) * part + index % part

    def tables(pair, carry):
        cols = pl.ds(pl.multiple_of(EMB + pair * 2 * EMB, EMB), 2 * EMB)
        shift = jnp.concatenate(
            [bias_ref[pl.ds(1 + 2 * pair, 1), :], bias_ref[pl.ds(2 + 2 * pair, 1), :]], axis=1
        )
        mixed = jnp.dot(r["hid"][...], r["u"][:, cols], preferred_element_type=f32) + shift
        back = jnp.dot(r["hgr"][...], r["v"][:, cols], preferred_element_type=f32)
        up_all = jnp.concatenate([r["up"][0, :, cols], r["up"][1, :, cols]], axis=0).astype(f32)
        pooled = (up_all * (1.0 + mixed) + back).astype(bf16)
        for piece in range(2):
            table = pair * 2 + piece
            owner, slot = place_ref[table], r["slot"][table]
            sums = jnp.zeros((2 * part, EMB), f32)
            for who in range(2):
                looked = r["ids"][who, owner, slot]
                count = jnp.zeros((2 * part, samples), f32)
                for k in range(looked.shape[0]):
                    count += jnp.where(looked[k : k + 1, :] == row_of, 1.0, 0.0)
                sums += jnp.dot(
                    count.astype(bf16),
                    pooled[who * samples : (who + 1) * samples, piece * EMB : (piece + 1) * EMB],
                    preferred_element_type=f32,
                )
            r["oc0"][table] = sums[:half]
            r["sc0"][table] = sums[part : part + half].astype(bf16)
            r["pt"][x, table] = sums[half:part]
            r["pt"][1 - x, table] = sums[part + half :]
        return carry

    mine.wait()
    for copy in id_copies:
        copy.wait()
    early = TABLES // 4
    lax.fori_loop(0, early, tables, 0)
    a1 = halve("a", 0, 2, y, g, yt, a0)
    lax.fori_loop(early, TABLES // 2, tables, 0)
    c0 = send("c", 0, xg, t)

    def each_slot(yy, put):
        def run(i, carry):
            owner = i // slots_dev * 2 + yy
            which = r["inv"][owner * slots_dev + i % slots_dev]
            there = jnp.where(which >= 0, 1.0, 0.0)
            z = i // slots_dev
            put((z // 2, z % 2, i % slots_dev), jnp.maximum(which, 0), there)
            return carry

        lax.fori_loop(0, slots_dev * n_tbl // 2, run, 0)

    def put_d(ref, kind):
        def put(at, which, there):
            for xx in range(2):
                ref[(xx, *at)] = (r["pt"][xx, which] * there).astype(kind)

        return put

    def put_c(ref, kind):
        def put(at, which, there):
            ref[at] = ((r["oc0"][which] + r["rc0"][which].astype(f32)) * there).astype(kind)

        return put

    each_slot(1 - y, put_d(r["sd0"], bf16))
    d0 = send("d", 0, g, yt)
    b1 = halve("b", 0, 0, x, xg, t, b0)
    each_slot(y, put_d(r["od0"], f32))
    a2 = halve("a", 1, 1, zl, g, zlt, a1)
    c0.wait()
    each_slot(1 - y, put_c(r["sc1"], bf16))
    c1 = send("c", 1, g, yt)
    each_slot(y, put_c(r["oc1"], f32))
    d1 = halve("d", 0, 0, x, xg, t, d0)
    a3 = halve("a", 2, 0, zh, g, zht, a2)
    b2 = halve("b", 1, 1, zl, g, zlt, b1)
    c2 = halve("c", 1, 1, zl, g, zlt, c1)
    d2 = halve("d", 1, 1, zl, g, zlt, d1)
    b3 = halve("b", 2, 0, zh, g, zht, b2)
    c3 = halve("c", 2, 0, zh, g, zht, c2)
    d3 = halve("d", 2, 0, zh, g, zht, d2)

    def total(name):
        return r["o%s3" % name][...] + r["r%s3" % name][...].astype(f32)

    def finish(value, lo, hi):
        value = value * scale
        cross_ref[:, lo:hi] = value[:8]
        cross_ref[:, width + lo : width + hi] = value[8:]

    a3.wait()
    finish(total("a"), 0, cut)
    b3.wait()
    finish(total("b"), cut, width)
    c3.wait()
    table_ref[:, :half, :] = total("c")
    d3.wait()
    table_ref[:, half:, :] = total("d")


def copy_body(cross_ref, table_ref, cross_out, table_out):
    cross_out[...] = cross_ref[...]
    table_out[...] = table_ref[...]


def on_device_fused(cross_input, upstream, v_weight, u_weight, bias, placement, owned_ids):
    n_grp = lax.axis_size("grp")
    n_tbl = lax.axis_size("tbl")
    samples, width = cross_input.shape
    rank = v_weight.shape[0]
    slots_dev, hot = owned_ids.shape[:2]
    scale = 1.0 / math.sqrt(samples * n_grp * n_tbl)
    part = ROWS // n_grp
    cut = (width // EMB // 2) * EMB
    scratch = scratch_of(samples, width, rank, n_tbl, slots_dev, hot, part, cut)
    vmem = pl.BlockSpec(memory_space=pltpu.VMEM)
    smem = pl.BlockSpec(memory_space=pltpu.SMEM)
    hbm = pl.BlockSpec(memory_space=pl.ANY)
    shapes = (
        jax.ShapeDtypeStruct((rank // (n_grp * n_tbl), 2 * width), jnp.float32),
        jax.ShapeDtypeStruct((slots_dev, part, EMB), jnp.float32),
    )
    sums = pl.pallas_call(
        functools.partial(fused_body, n_grp, n_tbl, scale, cut, tuple(scratch)),
        out_shape=shapes,
        in_specs=[hbm] * 4 + [vmem, smem, hbm],
        out_specs=(vmem, vmem),
        scratch_shapes=list(scratch.values()),
        compiler_params=pltpu.CompilerParams(
            collective_id=0, has_side_effects=True, vmem_limit_bytes=60 * 1024 * 1024
        ),
        name="cross_backward",
    )(
        cross_input, upstream, v_weight, u_weight,
        bias.reshape(width // EMB, EMB), placement, owned_ids,
    )
    return pl.pallas_call(
        copy_body,
        out_shape=shapes,
        in_specs=[vmem, vmem],
        out_specs=(vmem, vmem),
        name="hand_over",
    )(*sums)


def solution(mesh):
    in_specs = (
        P(("grp", "tbl"), None),
        P(("grp", "tbl"), None),
        P(),
        P(),
        P(),
        P(),
        P("tbl", None, "grp"),
    )
    out_specs = (P(("grp", "tbl"), None), P("tbl", "grp", None))
    fused = halving_fits(mesh.shape["grp"], mesh.shape["tbl"])
    return jax.shard_map(
        on_device_fused if fused else on_device, mesh=mesh, in_specs=in_specs, out_specs=out_specs, check_vma=False
    )
```

```python
import functools
import math

import jax
import jax.numpy as jnp
from jax import lax
from jax.experimental import pallas as pl
from jax.experimental.pallas import tpu as pltpu
from jax.sharding import PartitionSpec as P

EMB = 128
TABLES = 26
ROWS = 256
MESH = pl.DeviceIdType.MESH


def outer_sum(left, right):
    return jnp.einsum("br,bd->rd", left, right, preferred_element_type=jnp.float32)


def on_device(cross_input, upstream, v_weight, u_weight, bias, placement, owned_ids):
    n_grp = lax.axis_size("grp")
    n_tbl = lax.axis_size("tbl")
    samples = cross_input.shape[0]
    slots_dev = owned_ids.shape[0]
    scale = 1.0 / math.sqrt(samples * n_grp * n_tbl)
    hidden = jnp.dot(cross_input, v_weight.T, preferred_element_type=jnp.float32).astype(
        jnp.bfloat16
    )
    mixed = jnp.dot(hidden, u_weight, preferred_element_type=jnp.float32) + bias
    up_float = upstream.astype(jnp.float32)
    product_grad = (up_float * cross_input.astype(jnp.float32)).astype(jnp.bfloat16)
    hidden_grad = jnp.dot(product_grad, u_weight.T, preferred_element_type=jnp.float32).astype(
        jnp.bfloat16
    )
    input_grad = up_float * (1.0 + mixed) + jnp.dot(
        hidden_grad, v_weight, preferred_element_type=jnp.float32
    )
    pooled = input_grad[:, EMB:].astype(jnp.bfloat16).reshape(samples, TABLES, EMB)
    same = placement[:, None] == placement[None, :]
    earlier = jnp.arange(TABLES)[None, :] < jnp.arange(TABLES)[:, None]
    slot = jnp.sum((same & earlier).astype(jnp.int32), axis=1)
    target = slot * n_tbl + placement
    select = (jnp.arange(slots_dev * n_tbl, dtype=jnp.int32)[:, None] == target[None, :]).astype(
        jnp.bfloat16
    )
    outgoing = jnp.einsum("st,bte->sbe", select, pooled, preferred_element_type=jnp.float32)
    outgoing = outgoing.astype(jnp.bfloat16).reshape(slots_dev, n_tbl, samples, EMB)
    arriving = lax.all_to_all(outgoing, "tbl", split_axis=1, concat_axis=1, tiled=True)
    arriving = arriving.reshape(slots_dev, n_tbl * samples, EMB)
    row_numbers = jnp.arange(ROWS, dtype=jnp.int32)
    counts = jnp.sum(
        (owned_ids[:, :, None, :] == row_numbers[None, None, :, None]).astype(jnp.bfloat16), axis=1
    )
    row_terms = jnp.einsum("srm,sme->sre", counts, arriving, preferred_element_type=jnp.float32)
    table_grad = lax.psum_scatter(row_terms, "grp", scatter_dimension=1, tiled=True)
    term = jnp.concatenate(
        [outer_sum(hidden, product_grad), outer_sum(hidden_grad, cross_input)], axis=1
    )
    summed = lax.psum_scatter(term, ("grp", "tbl"), scatter_dimension=0, tiled=True)
    cross_grad = summed * scale
    return (cross_grad, table_grad)


def halving_fits(n_grp, n_tbl):
    return n_grp == 4 and n_tbl == 8


def scratch_of(samples, width, rank, n_tbl, slots_dev, hot, part, cuts):
    f32, bf16, i32 = jnp.float32, jnp.bfloat16, jnp.int32
    V, half = pltpu.VMEM, part // 2
    tab = (slots_dev, half, EMB)
    out = {
        "ci": V((2, samples, width), bf16),
        "up": V((2, samples, width), bf16),
        "v": V((rank, width), bf16),
        "u": V((rank, width), bf16),
        "pg": V((2, samples, width), bf16),
        "hid": V((2 * samples, rank), bf16),
        "hgr": V((2 * samples, rank), bf16),
        "hid_t": V((2, rank, samples), bf16),
        "hgr_t": V((2, rank, samples), bf16),
        "ids": V((2, n_tbl, slots_dev, hot, samples), i32),
        "slot": pltpu.SMEM((TABLES,), i32),
        "inv": pltpu.SMEM((slots_dev * n_tbl,), i32),
        "load_sem": pltpu.SemaphoreType.DMA((4,)),
        "in_s": pltpu.SemaphoreType.DMA((10,)),
        "in_r": pltpu.SemaphoreType.DMA((10,)),
        "id_s": pltpu.SemaphoreType.DMA((2, n_tbl)),
        "id_r": pltpu.SemaphoreType.DMA((2, n_tbl)),
        "ssem": pltpu.SemaphoreType.DMA((20,)),
        "rsem": pltpu.SemaphoreType.DMA((20,)),
    }
    lead = ((2, 2, 2), (2, 2), (2,), ())
    for name, tile in (
        ("a", (16, cuts[1] - cuts[0])),
        ("b", (16, cuts[2] - cuts[1])),
        ("e", (16, cuts[3] - cuts[2])),
        ("c", tab),
        ("d", tab),
    ):
        for k in range(4):
            shape = lead[k] + tile
            if name in "cd" and k == 0:
                shape = (TABLES, half, EMB)
            out["s%s%d" % (name, k)] = V(shape, bf16)
            out["r%s%d" % (name, k)] = V(shape, bf16)
            out["o%s%d" % (name, k)] = V(shape, f32)
    return out


def fused_body(n_grp, n_tbl, scale, cuts, names, *refs):
    f32, bf16 = jnp.float32, jnp.bfloat16
    ci_hbm, up_hbm, v_hbm, u_hbm, bias_ref, place_ref, ids_hbm, cross_ref, table_ref = refs[:9]
    r = dict(zip(names, refs[9:]))
    g = lax.axis_index("grp")
    t = lax.axis_index("tbl")
    core, x = g % 2, g // 2
    y, zl, zh = t % 2, (t // 2) % 2, t // 4
    og = g + 1 - 2 * core
    xg = core + 2 * (1 - x)
    yt = t + 1 - 2 * y
    zlt = t + 2 * (1 - 2 * zl)
    zht = t + 4 * (1 - 2 * zh)
    samples, width = ci_hbm.shape
    rank = v_hbm.shape[0]
    slots_dev = ids_hbm.shape[0]
    part = ROWS // n_grp
    half = part // 2

    barrier = pltpu.get_barrier_semaphore()

    def greet(gg, tt):
        pl.semaphore_signal(barrier, inc=1, device_id=(gg, tt), device_id_type=MESH)

    for step in range(1, n_tbl):
        greet(g, (t + step) % n_tbl)
        greet(og, (t + step) % n_tbl)
    greet(og, t)
    greet(xg, t)

    loads = [
        pltpu.make_async_copy(src, dst, r["load_sem"].at[i])
        for i, (src, dst) in enumerate(
            ((ci_hbm, r["ci"].at[0]), (v_hbm, r["v"]), (up_hbm, r["up"].at[0]), (u_hbm, r["u"]))
        )
    ]
    for load in loads:
        load.start()

    places = [place_ref[i] for i in range(TABLES)]
    targets = []
    for i in range(TABLES):
        slot = jnp.int32(0)
        for j in range(i):
            slot += (places[j] == places[i]).astype(jnp.int32)
        r["slot"][i] = jnp.minimum(slot, slots_dev - 1)
        targets.append(places[i] * slots_dev + slot)
    for q in range(slots_dev * n_tbl):
        which = jnp.int32(-1)
        for i in range(TABLES):
            which = jnp.where(targets[i] == q, i, which)
        r["inv"][q] = which

    nt = (((1,), (1,)), ((), ()))
    own_rows, their_rows = pl.ds(0, samples), pl.ds(samples, samples)
    loads[0].wait()
    loads[1].wait()
    hidden = lax.dot_general(r["ci"][0], r["v"][...], nt, preferred_element_type=f32)
    r["hid"][own_rows, :] = hidden.astype(bf16)
    r["hid_t"][0] = hidden.T.astype(bf16)
    loads[2].wait()
    loads[3].wait()
    r["pg"][0] = (r["up"][0].astype(f32) * r["ci"][0].astype(f32)).astype(bf16)
    hgrad = lax.dot_general(r["pg"][0], r["u"][...], nt, preferred_element_type=f32)
    r["hgr"][own_rows, :] = hgrad.astype(bf16)
    r["hgr_t"][0] = hgrad.T.astype(bf16)

    pl.semaphore_wait(barrier, 2 * n_tbl)

    def remote(src, dst, s, rs, gg, tt):
        copy = pltpu.make_async_remote_copy(
            src_ref=src, dst_ref=dst, send_sem=s, recv_sem=rs,
            device_id=(gg, tt), device_id_type=MESH,
        )
        copy.start()
        return copy

    pieces = [pl.ds(cuts[i], cuts[i + 1] - cuts[i]) for i in range(3)]
    moves = [(r["hid_t"].at[0], r["hid_t"].at[1]), (r["hgr_t"].at[0], r["hgr_t"].at[1])]
    for cols in pieces:
        moves.append((ci_hbm.at[:, cols], r["ci"].at[1, :, cols]))
        moves.append((up_hbm.at[:, cols], r["up"].at[1, :, cols]))
    moves.append((r["hid"].at[own_rows], r["hid"].at[their_rows]))
    moves.append((r["hgr"].at[own_rows], r["hgr"].at[their_rows]))
    in_copies = [
        remote(src, dst, r["in_s"].at[i], r["in_r"].at[i], og, t)
        for i, (src, dst) in enumerate(moves)
    ]
    id_copies = []
    for step in range(n_tbl):
        to = (t + step) % n_tbl
        block = ids_hbm.at[:, :, pl.ds(pl.multiple_of(to * samples, samples), samples)]
        if step == 0:
            mine = pltpu.make_async_copy(block, r["ids"].at[0, t], r["id_s"].at[0, 0])
            mine.start()
        else:
            id_copies.append(
                remote(block, r["ids"].at[0, t], r["id_s"].at[0, step], r["id_r"].at[0, step], g, to)
            )
        id_copies.append(
            remote(block, r["ids"].at[1, t], r["id_s"].at[1, step], r["id_r"].at[1, step], og, to)
        )

    quarter = rank // n_grp

    def picked(ref):
        both = []
        for who in range(2):
            for start in (core + 2 * x, core + 2 - 2 * x):
                at = pl.ds(pl.multiple_of(start * quarter, quarter), quarter)
                both.append(ref[who, at, :])
        return [jnp.concatenate(both[:2], axis=0), jnp.concatenate(both[2:], axis=0)]

    in_copies[0].wait()
    in_copies[1].wait()
    hsel, gsel = picked(r["hid_t"]), picked(r["hgr_t"])

    def blocks(lo, hi):
        theirs = r["ci"][1, :, lo:hi]
        product = (r["up"][1, :, lo:hi].astype(f32) * theirs.astype(f32)).astype(bf16)
        left = jnp.dot(hsel[0], r["pg"][0, :, lo:hi], preferred_element_type=f32)
        left += jnp.dot(hsel[1], product, preferred_element_type=f32)
        right = jnp.dot(gsel[0], r["ci"][0, :, lo:hi], preferred_element_type=f32)
        right += jnp.dot(gsel[1], theirs, preferred_element_type=f32)
        return [
            jnp.concatenate([left[8 * d : 8 * d + 8], right[8 * d : 8 * d + 8]], axis=0)
            for d in range(2 * n_tbl)
        ]

    in_copies[2].wait()
    in_copies[3].wait()
    for lo in range(cuts[0], cuts[1], 512):
        hi = min(lo + 512, cuts[1])
        made = blocks(lo, hi)
        for d in range(n_tbl):
            at = (d // 4, (d // 2) % 2, d % 2, slice(None), slice(lo, hi))
            r["oa0"][at] = made[d]
            r["sa0"][at] = made[n_tbl + d].astype(bf16)
    sems = iter(range(20))

    def send(name, k, gg, tt):
        i = next(sems)
        return remote(
            r["s%s%d" % (name, k)], r["r%s%d" % (name, k)], r["ssem"].at[i], r["rsem"].at[i], gg, tt
        )

    a0 = send("a", 0, xg, t)
    in_copies[4].wait()
    in_copies[5].wait()
    for lo in range(cuts[1], cuts[2], 512):
        hi = min(lo + 512, cuts[2])
        made = blocks(lo, hi)
        for side in range(2):
            xx = x if side == 0 else 1 - x
            for z in range(n_tbl // 2):
                even, odd = made[side * n_tbl + 2 * z], made[side * n_tbl + 2 * z + 1]
                at = (xx, z // 2, z % 2, slice(None), slice(lo - cuts[1], hi - cuts[1]))
                r["ob0"][at] = jnp.where(y == 0, even, odd)
                r["sb0"][at] = jnp.where(y == 0, odd, even).astype(bf16)
    b0 = send("b", 0, g, yt)
    in_copies[6].wait()
    in_copies[7].wait()
    for lo in range(cuts[2], cuts[3], 512):
        hi = min(lo + 512, cuts[3])
        made = blocks(lo, hi)
        for side in range(2):
            xx = x if side == 0 else 1 - x
            for z in range(2):
                for yy in range(2):
                    first = side * n_tbl + 4 * z + yy
                    at = (xx, z, yy, slice(None), slice(lo - cuts[2], hi - cuts[2]))
                    r["oe0"][at] = jnp.where(zl == 0, made[first], made[first + 2])
                    r["se0"][at] = jnp.where(zl == 0, made[first + 2], made[first]).astype(bf16)
    e0 = send("e", 0, g, zlt)

    def indices(depth):
        out = [()]
        for _ in range(depth):
            out = [i + (j,) for i in out for j in range(2)]
        return out

    def halve(name, k, axis, bit, gg, tt, before):
        before.wait()
        own, came = r["o%s%d" % (name, k)], r["r%s%d" % (name, k)]
        kept, out = r["o%s%d" % (name, k + 1)], r["s%s%d" % (name, k + 1)]

        def where_to(i, b):
            return i[:axis] + (b,) + i[axis:]

        def fill(dst, b, kind):
            for i in indices(2 - k):
                at = where_to(i, b)
                value = own[at] + came[at].astype(f32)
                if i:
                    dst[i] = value.astype(kind)
                else:
                    dst[...] = value.astype(kind)

        fill(out, 1 - bit, bf16)
        copy = send(name, k + 1, gg, tt)
        fill(kept, bit, f32)
        return copy

    index = lax.broadcasted_iota(jnp.int32, (2 * part, samples), 0)
    side_of = jnp.where(index // part == 0, x, 1 - x)
    row_of = (side_of * 2 + core) * part + index % part

    def tables(pair, carry):
        cols = pl.ds(pl.multiple_of(EMB + pair * 2 * EMB, EMB), 2 * EMB)
        shift = jnp.concatenate(
            [bias_ref[pl.ds(1 + 2 * pair, 1), :], bias_ref[pl.ds(2 + 2 * pair, 1), :]], axis=1
        )
        mixed = jnp.dot(r["hid"][...], r["u"][:, cols], preferred_element_type=f32) + shift
        back = jnp.dot(r["hgr"][...], r["v"][:, cols], preferred_element_type=f32)
        up_all = jnp.concatenate([r["up"][0, :, cols], r["up"][1, :, cols]], axis=0).astype(f32)
        pooled = (up_all * (1.0 + mixed) + back).astype(bf16)
        for piece in range(2):
            table = pair * 2 + piece
            owner, slot = place_ref[table], r["slot"][table]
            sums = jnp.zeros((2 * part, EMB), f32)
            for who in range(2):
                looked = r["ids"][who, owner, slot]
                count = jnp.zeros((2 * part, samples), f32)
                for k in range(looked.shape[0]):
                    count += jnp.where(looked[k : k + 1, :] == row_of, 1.0, 0.0)
                sums += jnp.dot(
                    count.astype(bf16),
                    pooled[who * samples : (who + 1) * samples, piece * EMB : (piece + 1) * EMB],
                    preferred_element_type=f32,
                )
            r["oc0"][table] = sums[:half]
            r["sc0"][table] = sums[part : part + half].astype(bf16)
            r["od0"][table] = sums[half:part]
            r["sd0"][table] = sums[part + half :].astype(bf16)
        return carry

    in_copies[8].wait()
    in_copies[9].wait()
    mine.wait()
    for copy in id_copies:
        copy.wait()
    lax.fori_loop(0, TABLES // 2, tables, 0)
    c0 = send("c", 0, xg, t)
    d0 = send("d", 0, xg, t)

    def each_slot(yy, put):
        def run(i, carry):
            owner = i // slots_dev * 2 + yy
            which = r["inv"][owner * slots_dev + i % slots_dev]
            there = jnp.where(which >= 0, 1.0, 0.0)
            z = i // slots_dev
            put((z // 2, z % 2, i % slots_dev), jnp.maximum(which, 0), there)
            return carry

        lax.fori_loop(0, slots_dev * n_tbl // 2, run, 0)

    def put(name, dst, kind):
        def store(at, which, there):
            value = r["o%s0" % name][which] + r["r%s0" % name][which].astype(f32)
            dst[at] = (value * there).astype(kind)

        return store

    def spread(name, before):
        before.wait()
        each_slot(1 - y, put(name, r["s%s1" % name], bf16))
        copy = send(name, 1, g, yt)
        each_slot(y, put(name, r["o%s1" % name], f32))
        return copy

    a1 = halve("a", 0, 2, y, g, yt, a0)
    e1 = halve("e", 0, 1, zh, g, zht, e0)
    b1 = halve("b", 0, 0, x, xg, t, b0)
    c1 = spread("c", c0)
    a2 = halve("a", 1, 1, zl, g, zlt, a1)
    e2 = halve("e", 1, 0, x, xg, t, e1)
    d1 = spread("d", d0)
    b2 = halve("b", 1, 1, zl, g, zlt, b1)
    a3 = halve("a", 2, 0, zh, g, zht, a2)
    c2 = halve("c", 1, 1, zl, g, zlt, c1)
    e3 = halve("e", 2, 0, y, g, yt, e2)
    b3 = halve("b", 2, 0, zh, g, zht, b2)
    d2 = halve("d", 1, 1, zl, g, zlt, d1)
    c3 = halve("c", 2, 0, zh, g, zht, c2)
    d3 = halve("d", 2, 0, zh, g, zht, d2)

    def total(name):
        return r["o%s3" % name][...] + r["r%s3" % name][...].astype(f32)

    def finish(value, lo, hi):
        value = value * scale
        cross_ref[:, lo:hi] = value[:8]
        cross_ref[:, width + lo : width + hi] = value[8:]

    for name, copy, i in (("a", a3, 0), ("b", b3, 1), ("e", e3, 2)):
        copy.wait()
        finish(total(name), cuts[i], cuts[i + 1])
    c3.wait()
    table_ref[:, :half, :] = total("c")
    d3.wait()
    table_ref[:, half:, :] = total("d")


def copy_body(cross_ref, table_ref, cross_out, table_out):
    cross_out[...] = cross_ref[...]
    table_out[...] = table_ref[...]


def on_device_fused(cross_input, upstream, v_weight, u_weight, bias, placement, owned_ids):
    n_grp = lax.axis_size("grp")
    n_tbl = lax.axis_size("tbl")
    samples, width = cross_input.shape
    rank = v_weight.shape[0]
    slots_dev, hot = owned_ids.shape[:2]
    scale = 1.0 / math.sqrt(samples * n_grp * n_tbl)
    part = ROWS // n_grp
    tiles = width // EMB
    cuts = (0, tiles * 7 // 27 * EMB, tiles * 18 // 27 * EMB, width)
    scratch = scratch_of(samples, width, rank, n_tbl, slots_dev, hot, part, cuts)
    vmem = pl.BlockSpec(memory_space=pltpu.VMEM)
    smem = pl.BlockSpec(memory_space=pltpu.SMEM)
    hbm = pl.BlockSpec(memory_space=pl.ANY)
    shapes = (
        jax.ShapeDtypeStruct((rank // (n_grp * n_tbl), 2 * width), jnp.float32),
        jax.ShapeDtypeStruct((slots_dev, part, EMB), jnp.float32),
    )
    sums = pl.pallas_call(
        functools.partial(fused_body, n_grp, n_tbl, scale, cuts, tuple(scratch)),
        out_shape=shapes,
        in_specs=[hbm] * 4 + [vmem, smem, hbm],
        out_specs=(vmem, vmem),
        scratch_shapes=list(scratch.values()),
        compiler_params=pltpu.CompilerParams(
            collective_id=0, has_side_effects=True, vmem_limit_bytes=60 * 1024 * 1024
        ),
        name="cross_backward",
    )(
        cross_input, upstream, v_weight, u_weight,
        bias.reshape(width // EMB, EMB), placement, owned_ids,
    )
    return pl.pallas_call(
        copy_body,
        out_shape=shapes,
        in_specs=[vmem, vmem],
        out_specs=(vmem, vmem),
        name="hand_over",
    )(*sums)


def solution(mesh):
    in_specs = (
        P(("grp", "tbl"), None),
        P(("grp", "tbl"), None),
        P(),
        P(),
        P(),
        P(),
        P("tbl", None, "grp"),
    )
    out_specs = (P(("grp", "tbl"), None), P("tbl", "grp", None))
    fused = halving_fits(mesh.shape["grp"], mesh.shape["tbl"])
    return jax.shard_map(
        on_device_fused if fused else on_device, mesh=mesh, in_specs=in_specs, out_specs=out_specs, check_vma=False
    )
```

```python
import functools
import math

import jax
import jax.numpy as jnp
from jax import lax
from jax.experimental import pallas as pl
from jax.experimental.pallas import tpu as pltpu
from jax.sharding import PartitionSpec as P

EMB = 128
TABLES = 26
ROWS = 256
MESH = pl.DeviceIdType.MESH


def outer_sum(left, right):
    return jnp.einsum("br,bd->rd", left, right, preferred_element_type=jnp.float32)


def on_device(cross_input, upstream, v_weight, u_weight, bias, placement, owned_ids):
    n_grp = lax.axis_size("grp")
    n_tbl = lax.axis_size("tbl")
    samples = cross_input.shape[0]
    slots_dev = owned_ids.shape[0]
    scale = 1.0 / math.sqrt(samples * n_grp * n_tbl)
    hidden = jnp.dot(cross_input, v_weight.T, preferred_element_type=jnp.float32).astype(
        jnp.bfloat16
    )
    mixed = jnp.dot(hidden, u_weight, preferred_element_type=jnp.float32) + bias
    up_float = upstream.astype(jnp.float32)
    product_grad = (up_float * cross_input.astype(jnp.float32)).astype(jnp.bfloat16)
    hidden_grad = jnp.dot(product_grad, u_weight.T, preferred_element_type=jnp.float32).astype(
        jnp.bfloat16
    )
    input_grad = up_float * (1.0 + mixed) + jnp.dot(
        hidden_grad, v_weight, preferred_element_type=jnp.float32
    )
    pooled = input_grad[:, EMB:].astype(jnp.bfloat16).reshape(samples, TABLES, EMB)
    same = placement[:, None] == placement[None, :]
    earlier = jnp.arange(TABLES)[None, :] < jnp.arange(TABLES)[:, None]
    slot = jnp.sum((same & earlier).astype(jnp.int32), axis=1)
    target = slot * n_tbl + placement
    select = (jnp.arange(slots_dev * n_tbl, dtype=jnp.int32)[:, None] == target[None, :]).astype(
        jnp.bfloat16
    )
    outgoing = jnp.einsum("st,bte->sbe", select, pooled, preferred_element_type=jnp.float32)
    outgoing = outgoing.astype(jnp.bfloat16).reshape(slots_dev, n_tbl, samples, EMB)
    arriving = lax.all_to_all(outgoing, "tbl", split_axis=1, concat_axis=1, tiled=True)
    arriving = arriving.reshape(slots_dev, n_tbl * samples, EMB)
    row_numbers = jnp.arange(ROWS, dtype=jnp.int32)
    counts = jnp.sum(
        (owned_ids[:, :, None, :] == row_numbers[None, None, :, None]).astype(jnp.bfloat16), axis=1
    )
    row_terms = jnp.einsum("srm,sme->sre", counts, arriving, preferred_element_type=jnp.float32)
    table_grad = lax.psum_scatter(row_terms, "grp", scatter_dimension=1, tiled=True)
    term = jnp.concatenate(
        [outer_sum(hidden, product_grad), outer_sum(hidden_grad, cross_input)], axis=1
    )
    summed = lax.psum_scatter(term, ("grp", "tbl"), scatter_dimension=0, tiled=True)
    cross_grad = summed * scale
    return (cross_grad, table_grad)


def halving_fits(n_grp, n_tbl):
    return n_grp == 4 and n_tbl == 8


def scratch_of(samples, width, rank, n_tbl, slots_dev, hot, part, cuts):
    f32, bf16, i32 = jnp.float32, jnp.bfloat16, jnp.int32
    V, half = pltpu.VMEM, part // 2
    tab = (slots_dev, half, EMB)
    out = {
        "ci": V((2, samples, width), bf16),
        "up": V((2, samples, width), bf16),
        "v": V((rank, width), bf16),
        "u": V((rank, width), bf16),
        "pg": V((2, samples, width), bf16),
        "hid": V((2 * samples, rank), bf16),
        "hgr": V((2 * samples, rank), bf16),
        "hid_t": V((2, rank, samples), bf16),
        "hgr_t": V((2, rank, samples), bf16),
        "ids": V((2, n_tbl, slots_dev, hot, samples), i32),
        "slot": pltpu.SMEM((TABLES,), i32),
        "inv": pltpu.SMEM((slots_dev * n_tbl,), i32),
        "load_sem": pltpu.SemaphoreType.DMA((4,)),
        "in_s": pltpu.SemaphoreType.DMA((10,)),
        "in_r": pltpu.SemaphoreType.DMA((10,)),
        "id_s": pltpu.SemaphoreType.DMA((2, n_tbl)),
        "id_r": pltpu.SemaphoreType.DMA((2, n_tbl)),
        "ssem": pltpu.SemaphoreType.DMA((20,)),
        "rsem": pltpu.SemaphoreType.DMA((20,)),
    }
    lead = ((2, 2, 2), (2, 2), (2,), ())
    for name, tile in (
        ("a", (16, cuts[1] - cuts[0])),
        ("b", (16, cuts[2] - cuts[1])),
        ("e", (16, cuts[3] - cuts[2])),
        ("c", tab),
        ("d", tab),
    ):
        for k in range(4):
            shape = lead[k] + tile
            if name in "cd" and k == 0:
                shape = (TABLES, half, EMB)
            out["s%s%d" % (name, k)] = V(shape, bf16)
            out["r%s%d" % (name, k)] = V(shape, bf16)
            out["o%s%d" % (name, k)] = V(shape, f32)
    return out


def fused_body(n_grp, n_tbl, scale, cuts, names, *refs):
    f32, bf16 = jnp.float32, jnp.bfloat16
    ci_hbm, up_hbm, v_hbm, u_hbm, bias_ref, place_ref, ids_hbm, cross_ref, table_ref = refs[:9]
    r = dict(zip(names, refs[9:]))
    g = lax.axis_index("grp")
    t = lax.axis_index("tbl")
    core, x = g % 2, g // 2
    y, zl, zh = t % 2, (t // 2) % 2, t // 4
    og = g + 1 - 2 * core
    xg = core + 2 * (1 - x)
    yt = t + 1 - 2 * y
    zlt = t + 2 * (1 - 2 * zl)
    zht = t + 4 * (1 - 2 * zh)
    samples, width = ci_hbm.shape
    rank = v_hbm.shape[0]
    slots_dev = ids_hbm.shape[0]
    part = ROWS // n_grp
    half = part // 2

    barrier = pltpu.get_barrier_semaphore()

    def greet(gg, tt):
        pl.semaphore_signal(barrier, inc=1, device_id=(gg, tt), device_id_type=MESH)

    for step in range(1, n_tbl):
        greet(g, (t + step) % n_tbl)
        greet(og, (t + step) % n_tbl)
    greet(og, t)
    greet(xg, t)

    loads = [
        pltpu.make_async_copy(src, dst, r["load_sem"].at[i])
        for i, (src, dst) in enumerate(
            ((ci_hbm, r["ci"].at[0]), (v_hbm, r["v"]), (up_hbm, r["up"].at[0]), (u_hbm, r["u"]))
        )
    ]
    for load in loads:
        load.start()

    places = [place_ref[i] for i in range(TABLES)]
    targets = []
    for i in range(TABLES):
        slot = jnp.int32(0)
        for j in range(i):
            slot += (places[j] == places[i]).astype(jnp.int32)
        r["slot"][i] = jnp.minimum(slot, slots_dev - 1)
        targets.append(places[i] * slots_dev + slot)
    for q in range(slots_dev * n_tbl):
        which = jnp.int32(-1)
        for i in range(TABLES):
            which = jnp.where(targets[i] == q, i, which)
        r["inv"][q] = which

    nt = (((1,), (1,)), ((), ()))
    own_rows, their_rows = pl.ds(0, samples), pl.ds(samples, samples)
    loads[0].wait()
    loads[1].wait()
    hidden = lax.dot_general(r["ci"][0], r["v"][...], nt, preferred_element_type=f32)
    r["hid"][own_rows, :] = hidden.astype(bf16)
    r["hid_t"][0] = hidden.T.astype(bf16)
    loads[2].wait()
    loads[3].wait()
    r["pg"][0] = (r["up"][0].astype(f32) * r["ci"][0].astype(f32)).astype(bf16)
    hgrad = lax.dot_general(r["pg"][0], r["u"][...], nt, preferred_element_type=f32)
    r["hgr"][own_rows, :] = hgrad.astype(bf16)
    r["hgr_t"][0] = hgrad.T.astype(bf16)

    pl.semaphore_wait(barrier, 2 * n_tbl)

    def remote(src, dst, s, rs, gg, tt):
        copy = pltpu.make_async_remote_copy(
            src_ref=src, dst_ref=dst, send_sem=s, recv_sem=rs,
            device_id=(gg, tt), device_id_type=MESH,
        )
        copy.start()
        return copy

    pieces = [pl.ds(cuts[i], cuts[i + 1] - cuts[i]) for i in range(3)]
    moves = [(r["hid_t"].at[0], r["hid_t"].at[1]), (r["hgr_t"].at[0], r["hgr_t"].at[1])]
    for cols in pieces:
        moves.append((ci_hbm.at[:, cols], r["ci"].at[1, :, cols]))
        moves.append((up_hbm.at[:, cols], r["up"].at[1, :, cols]))
    moves.append((r["hid"].at[own_rows], r["hid"].at[their_rows]))
    moves.append((r["hgr"].at[own_rows], r["hgr"].at[their_rows]))
    in_copies = [
        remote(src, dst, r["in_s"].at[i], r["in_r"].at[i], og, t)
        for i, (src, dst) in enumerate(moves)
    ]
    id_copies = []
    for step in range(n_tbl):
        to = (t + step) % n_tbl
        block = ids_hbm.at[:, :, pl.ds(pl.multiple_of(to * samples, samples), samples)]
        if step == 0:
            mine = pltpu.make_async_copy(block, r["ids"].at[0, t], r["id_s"].at[0, 0])
            mine.start()
        else:
            id_copies.append(
                remote(block, r["ids"].at[0, t], r["id_s"].at[0, step], r["id_r"].at[0, step], g, to)
            )
        id_copies.append(
            remote(block, r["ids"].at[1, t], r["id_s"].at[1, step], r["id_r"].at[1, step], og, to)
        )

    quarter = rank // n_grp

    def picked(ref):
        both = []
        for who in range(2):
            for start in (core + 2 * x, core + 2 - 2 * x):
                at = pl.ds(pl.multiple_of(start * quarter, quarter), quarter)
                both.append(ref[who, at, :])
        return [jnp.concatenate(both[:2], axis=0), jnp.concatenate(both[2:], axis=0)]

    in_copies[0].wait()
    in_copies[1].wait()
    hsel, gsel = picked(r["hid_t"]), picked(r["hgr_t"])

    def blocks(lo, hi):
        theirs = r["ci"][1, :, lo:hi]
        product = (r["up"][1, :, lo:hi].astype(f32) * theirs.astype(f32)).astype(bf16)
        left = jnp.dot(hsel[0], r["pg"][0, :, lo:hi], preferred_element_type=f32)
        left += jnp.dot(hsel[1], product, preferred_element_type=f32)
        right = jnp.dot(gsel[0], r["ci"][0, :, lo:hi], preferred_element_type=f32)
        right += jnp.dot(gsel[1], theirs, preferred_element_type=f32)
        return [
            jnp.concatenate([left[8 * d : 8 * d + 8], right[8 * d : 8 * d + 8]], axis=0)
            for d in range(2 * n_tbl)
        ]

    in_copies[2].wait()
    in_copies[3].wait()
    for lo in range(cuts[0], cuts[1], 512):
        hi = min(lo + 512, cuts[1])
        made = blocks(lo, hi)
        for d in range(n_tbl):
            at = (d // 4, (d // 2) % 2, d % 2, slice(None), slice(lo, hi))
            r["oa0"][at] = made[d]
            r["sa0"][at] = made[n_tbl + d].astype(bf16)
    sems = iter(range(20))

    def send(name, k, gg, tt):
        i = next(sems)
        return remote(
            r["s%s%d" % (name, k)], r["r%s%d" % (name, k)], r["ssem"].at[i], r["rsem"].at[i], gg, tt
        )

    a0 = send("a", 0, xg, t)
    in_copies[4].wait()
    in_copies[5].wait()
    for lo in range(cuts[1], cuts[2], 512):
        hi = min(lo + 512, cuts[2])
        made = blocks(lo, hi)
        for side in range(2):
            xx = x if side == 0 else 1 - x
            for z in range(n_tbl // 2):
                even, odd = made[side * n_tbl + 2 * z], made[side * n_tbl + 2 * z + 1]
                at = (xx, z // 2, z % 2, slice(None), slice(lo - cuts[1], hi - cuts[1]))
                r["ob0"][at] = jnp.where(y == 0, even, odd)
                r["sb0"][at] = jnp.where(y == 0, odd, even).astype(bf16)
    b0 = send("b", 0, g, yt)
    in_copies[6].wait()
    in_copies[7].wait()
    for lo in range(cuts[2], cuts[3], 512):
        hi = min(lo + 512, cuts[3])
        made = blocks(lo, hi)
        for side in range(2):
            xx = x if side == 0 else 1 - x
            for z in range(2):
                for yy in range(2):
                    first = side * n_tbl + 4 * z + yy
                    at = (xx, z, yy, slice(None), slice(lo - cuts[2], hi - cuts[2]))
                    r["oe0"][at] = jnp.where(zl == 0, made[first], made[first + 2])
                    r["se0"][at] = jnp.where(zl == 0, made[first + 2], made[first]).astype(bf16)
    e0 = send("e", 0, g, zlt)

    def indices(depth):
        out = [()]
        for _ in range(depth):
            out = [i + (j,) for i in out for j in range(2)]
        return out

    def halve(name, k, axis, bit, gg, tt, before):
        before.wait()
        own, came = r["o%s%d" % (name, k)], r["r%s%d" % (name, k)]
        kept, out = r["o%s%d" % (name, k + 1)], r["s%s%d" % (name, k + 1)]

        def where_to(i, b):
            return i[:axis] + (b,) + i[axis:]

        def fill(dst, b, kind):
            for i in indices(2 - k):
                at = where_to(i, b)
                value = own[at] + came[at].astype(f32)
                if i:
                    dst[i] = value.astype(kind)
                else:
                    dst[...] = value.astype(kind)

        fill(out, 1 - bit, bf16)
        copy = send(name, k + 1, gg, tt)
        fill(kept, bit, f32)
        return copy

    index = lax.broadcasted_iota(jnp.int32, (2 * part, samples), 0)
    side_of = jnp.where(index // part == 0, x, 1 - x)
    row_of = (side_of * 2 + core) * part + index % part

    def tables(pair, carry):
        cols = pl.ds(pl.multiple_of(EMB + pair * 2 * EMB, EMB), 2 * EMB)
        shift = jnp.concatenate(
            [bias_ref[pl.ds(1 + 2 * pair, 1), :], bias_ref[pl.ds(2 + 2 * pair, 1), :]], axis=1
        )
        mixed = jnp.dot(r["hid"][...], r["u"][:, cols], preferred_element_type=f32) + shift
        back = jnp.dot(r["hgr"][...], r["v"][:, cols], preferred_element_type=f32)
        up_all = jnp.concatenate([r["up"][0, :, cols], r["up"][1, :, cols]], axis=0).astype(f32)
        pooled = (up_all * (1.0 + mixed) + back).astype(bf16)
        for piece in range(2):
            table = pair * 2 + piece
            owner, slot = place_ref[table], r["slot"][table]
            sums = jnp.zeros((2 * part, EMB), f32)
            for who in range(2):
                looked = r["ids"][who, owner, slot]
                count = jnp.zeros((2 * part, samples), f32)
                for k in range(looked.shape[0]):
                    count += jnp.where(looked[k : k + 1, :] == row_of, 1.0, 0.0)
                sums += jnp.dot(
                    count.astype(bf16),
                    pooled[who * samples : (who + 1) * samples, piece * EMB : (piece + 1) * EMB],
                    preferred_element_type=f32,
                )
            r["oc0"][table] = sums[:half]
            r["sc0"][table] = sums[part : part + half].astype(bf16)
            r["od0"][table] = sums[half:part]
            r["sd0"][table] = sums[part + half :].astype(bf16)
        return carry

    in_copies[8].wait()
    in_copies[9].wait()
    mine.wait()
    for copy in id_copies:
        copy.wait()
    lax.fori_loop(0, TABLES // 2, tables, 0)
    c0 = send("c", 0, xg, t)
    d0 = send("d", 0, xg, t)

    def each_slot(yy, put):
        def run(i, carry):
            owner = i // slots_dev * 2 + yy
            which = r["inv"][owner * slots_dev + i % slots_dev]
            there = jnp.where(which >= 0, 1.0, 0.0)
            z = i // slots_dev
            put((z // 2, z % 2, i % slots_dev), jnp.maximum(which, 0), there)
            return carry

        lax.fori_loop(0, slots_dev * n_tbl // 2, run, 0)

    def put(name, dst, kind):
        def store(at, which, there):
            value = r["o%s0" % name][which] + r["r%s0" % name][which].astype(f32)
            dst[at] = (value * there).astype(kind)

        return store

    def spread(name, before):
        before.wait()
        each_slot(1 - y, put(name, r["s%s1" % name], bf16))
        copy = send(name, 1, g, yt)
        each_slot(y, put(name, r["o%s1" % name], f32))
        return copy

    a1 = halve("a", 0, 2, y, g, yt, a0)
    e1 = halve("e", 0, 1, zh, g, zht, e0)
    b1 = halve("b", 0, 0, x, xg, t, b0)
    c1 = spread("c", c0)
    a2 = halve("a", 1, 1, zl, g, zlt, a1)
    e2 = halve("e", 1, 0, x, xg, t, e1)
    d1 = spread("d", d0)
    a3 = halve("a", 2, 0, zh, g, zht, a2)
    c2 = halve("c", 1, 1, zl, g, zlt, c1)
    b2 = halve("b", 1, 1, zl, g, zlt, b1)
    e3 = halve("e", 2, 0, y, g, yt, e2)
    d2 = halve("d", 1, 1, zl, g, zlt, d1)
    c3 = halve("c", 2, 0, zh, g, zht, c2)
    b3 = halve("b", 2, 0, zh, g, zht, b2)
    d3 = halve("d", 2, 0, zh, g, zht, d2)

    def total(name):
        return r["o%s3" % name][...] + r["r%s3" % name][...].astype(f32)

    def finish(value, lo, hi):
        value = value * scale
        cross_ref[:, lo:hi] = value[:8]
        cross_ref[:, width + lo : width + hi] = value[8:]

    for name, copy, i in (("a", a3, 0), ("b", b3, 1), ("e", e3, 2)):
        copy.wait()
        finish(total(name), cuts[i], cuts[i + 1])
    c3.wait()
    table_ref[:, :half, :] = total("c")
    d3.wait()
    table_ref[:, half:, :] = total("d")


def copy_body(cross_ref, table_ref, cross_out, table_out):
    cross_out[...] = cross_ref[...]
    table_out[...] = table_ref[...]


def on_device_fused(cross_input, upstream, v_weight, u_weight, bias, placement, owned_ids):
    n_grp = lax.axis_size("grp")
    n_tbl = lax.axis_size("tbl")
    samples, width = cross_input.shape
    rank = v_weight.shape[0]
    slots_dev, hot = owned_ids.shape[:2]
    scale = 1.0 / math.sqrt(samples * n_grp * n_tbl)
    part = ROWS // n_grp
    tiles = width // EMB
    cuts = (0, tiles * 7 // 27 * EMB, tiles * 18 // 27 * EMB, width)
    scratch = scratch_of(samples, width, rank, n_tbl, slots_dev, hot, part, cuts)
    vmem = pl.BlockSpec(memory_space=pltpu.VMEM)
    smem = pl.BlockSpec(memory_space=pltpu.SMEM)
    hbm = pl.BlockSpec(memory_space=pl.ANY)
    shapes = (
        jax.ShapeDtypeStruct((rank // (n_grp * n_tbl), 2 * width), jnp.float32),
        jax.ShapeDtypeStruct((slots_dev, part, EMB), jnp.float32),
    )
    sums = pl.pallas_call(
        functools.partial(fused_body, n_grp, n_tbl, scale, cuts, tuple(scratch)),
        out_shape=shapes,
        in_specs=[hbm] * 4 + [vmem, smem, hbm],
        out_specs=(vmem, vmem),
        scratch_shapes=list(scratch.values()),
        compiler_params=pltpu.CompilerParams(
            collective_id=0, has_side_effects=True, vmem_limit_bytes=60 * 1024 * 1024
        ),
        name="cross_backward",
    )(
        cross_input, upstream, v_weight, u_weight,
        bias.reshape(width // EMB, EMB), placement, owned_ids,
    )
    return pl.pallas_call(
        copy_body,
        out_shape=shapes,
        in_specs=[vmem, vmem],
        out_specs=(vmem, vmem),
        name="hand_over",
    )(*sums)


def solution(mesh):
    in_specs = (
        P(("grp", "tbl"), None),
        P(("grp", "tbl"), None),
        P(),
        P(),
        P(),
        P(),
        P("tbl", None, "grp"),
    )
    out_specs = (P(("grp", "tbl"), None), P("tbl", "grp", None))
    fused = halving_fits(mesh.shape["grp"], mesh.shape["tbl"])
    return jax.shard_map(
        on_device_fused if fused else on_device, mesh=mesh, in_specs=in_specs, out_specs=out_specs, check_vma=False
    )
```
